32 devices in a mesh: dp: 4 (over x, core), seq: 8 (over z, y).
Axes of the slice: x: 2, y: 2, z: 4, core: 2. Of those that a mesh axis runs over, the one named last changes fastest.
Arguments:
- hidden: bfloat16 [4, 1024, 2432], P('dp', 'seq'), may hold values from -6 to 6
- out_cot: bfloat16 [4, 1024, 2432], P('dp', 'seq'), may hold values from -6 to 6
- proj_in: bfloat16 [2432, 4096], P(None, 'dp'), may hold values from -0.125 to 0.125
- proj_out: bfloat16 [4096, 1536], P('dp'), may hold values from -0.09375 to 0.09375
- attn_out_w: bfloat16 [2048, 2432], replicated, may hold values from -0.125 to 0.125
- queries: bfloat16 [4, 1024, 2048], P('dp', 'seq'), as said below
- keys: bfloat16 [4, 1024, 2048], P('dp', 'seq'), as said below
- values: bfloat16 [4, 1024, 2048], P('dp', 'seq'), may hold values from -6 to 6
- dino: bfloat16 [4, 1536, 1024], P('dp', 'seq'), as said below
Outputs:
- cosine: float32 [4, 1024], P('dp', 'seq')
- grad_queries: bfloat16 [4, 1024, 2048], P('dp', 'seq')
- grad_keys: bfloat16 [4, 1024, 2048], P('dp', 'seq')
- grad_values: bfloat16 [4, 1024, 2048], P('dp', 'seq')
The draws below stay inside these ranges and needn't reach their ends.
Inputs may be any that keep to these rules, and one draw needn't show every extreme that they name: `dino`: real-valued features, channels of differing scale and offset. real-valued queries. real-valued keys.
All inputs are finite; a program needn't handle non-finite values.
Results may differ from the reference program's by a relative error of at most 0.014.
Values may be sent and summed in bfloat16 or wider, within the bound.
No kernel may reach another device: no remote copies, remote signals or barrier semaphores. Data moves between devices by JAX's collectives and lax.ppermute only.
A program may use at most 128 MiB of HBM per device.

```python
import jax
import jax.numpy as jnp
from jax import lax

D = 2432
PROJ_HID = 4096
D_DINO = 1536
HEADS = 32
HEAD_DIM = 64
IMAGES = 4
TOKENS = 1024


def query_key_pair(key):
    shape = (IMAGES, TOKENS, HEADS * HEAD_DIM)
    base = jax.random.fold_in(key, 4711)
    key_query, key_keys = jax.random.split(base, 2)
    query_draw = jax.random.truncated_normal(key_query, -4.0, 4.0, shape, jnp.float32)
    key_draw = jax.random.truncated_normal(key_keys, -4.0, 4.0, shape, jnp.float32)
    return (query_draw, key_draw)


def draw_queries(key, part):
    return query_key_pair(key)[0].astype(jnp.bfloat16)


def draw_keys(key, part):
    return query_key_pair(key)[1].astype(jnp.bfloat16)


def draw_dino(key, part):
    key_base, key_scale, key_shift = jax.random.split(jax.random.fold_in(key, 911), 3)
    base = jax.random.normal(key_base, (IMAGES, D_DINO, TOKENS), jnp.float32)
    channel_scale = jnp.exp(jax.random.uniform(key_scale, (1, D_DINO, 1), jnp.float32, 0.0, 2.302585))
    channel_shift = 2.0 * jax.random.normal(key_shift, (1, D_DINO, 1), jnp.float32)
    features = base * channel_scale + channel_shift
    return features.astype(jnp.bfloat16)


def block_scale(key, dims, pieces, low, largest):
    factor_of, own = 1.0, jax.random.fold_in(key, 6)
    for axis_at, blocks in pieces:
        steps = jnp.exp(jax.random.uniform(jax.random.fold_in(own, axis_at), (blocks,), jnp.float32, low / len(pieces), largest / len(pieces)))
        factor_of = factor_of * jnp.repeat(steps, dims[axis_at] // blocks).reshape([-1 if axis == axis_at else 1 for axis in range(len(dims))])
    return factor_of


def scatter_about(rng, extent, scale, most, shards=(), held_as=jnp.bfloat16):
    gain = block_scale(rng, extent, shards, -0.22, 0.18) if shards else 1.0
    entries = jax.random.normal(rng, extent, jnp.float32) * scale * gain
    return jnp.minimum(jnp.maximum(entries, -most), most).astype(held_as)


def setup_inputs(seed: int = 0) -> dict:
    arg_keys = jax.random.split(jax.random.key(seed), 10)
    hidden = scatter_about(arg_keys[0], (IMAGES, TOKENS, D), 1.0, 6.0, ((0, 4), (1, 8)))
    out_cot = scatter_about(arg_keys[1], (IMAGES, TOKENS, D), 1.0, 6.0, ((0, 4), (1, 8)))
    proj_in = scatter_about(arg_keys[2], (D, PROJ_HID), D ** -0.5, 0.125, ((1, 4),))
    proj_out = scatter_about(arg_keys[3], (PROJ_HID, D_DINO), PROJ_HID ** -0.5, 0.09375, ((0, 4),))
    attn_out_w = scatter_about(arg_keys[4], (HEADS * HEAD_DIM, D), (HEADS * HEAD_DIM) ** -0.5, 0.125)
    queries = draw_queries(jax.random.fold_in(arg_keys[9], 71), 0)
    keys = draw_keys(jax.random.fold_in(arg_keys[9], 71), 0)
    values = scatter_about(arg_keys[7], (IMAGES, TOKENS, HEADS * HEAD_DIM), 1.0, 6.0, ((0, 4), (1, 8)))
    dino = draw_dino(jax.random.fold_in(arg_keys[9], 71), 0)
    return dict(hidden=hidden, out_cot=out_cot, proj_in=proj_in, proj_out=proj_out, attn_out_w=attn_out_w, queries=queries, keys=keys, values=values, dino=dino)


loss_weight = 1000.0

def unit_target(features):
    values32 = features.astype(jnp.float32)
    center = lax.optimization_barrier(jnp.mean(values32, axis=1, keepdims=True))
    shifted = values32 - center
    spread = lax.optimization_barrier(jnp.mean(shifted * shifted, axis=1, keepdims=True))
    normed = shifted * lax.rsqrt(spread + 1e-06)
    unit = normed * lax.rsqrt(lax.optimization_barrier(jnp.sum(normed * normed, axis=1, keepdims=True)) + 1e-06)
    return jnp.transpose(unit, (0, 2, 1))

def cosine_grad(projected, target):
    rinv = lax.rsqrt(lax.optimization_barrier(jnp.sum(projected * projected, axis=-1, keepdims=True)) + 1e-06)
    direction = projected * rinv
    cosine = lax.optimization_barrier(jnp.sum(direction * target, axis=-1))
    grad_z = -loss_weight * rinv * (target - cosine[..., None] * direction)
    return (cosine, grad_z.astype(jnp.bfloat16))

def silu_slope(pre_act):
    sigma = jax.nn.sigmoid(pre_act)
    return sigma * (1.0 + pre_act * (1.0 - sigma))

def head_backward(operands):
    query, key_rows, value_rows, grad_out = operands
    scale = HEAD_DIM ** (-0.5)
    scores = jnp.dot(query, key_rows.T, preferred_element_type=jnp.float32) * scale
    probs = jax.nn.softmax(scores, axis=-1)
    probs_b = probs.astype(jnp.bfloat16)
    attended = jnp.dot(probs_b, value_rows, preferred_element_type=jnp.float32)
    row_dot = lax.optimization_barrier(jnp.sum(grad_out.astype(jnp.float32) * attended, axis=-1, keepdims=True))
    grad_p = jnp.dot(grad_out, value_rows.T, preferred_element_type=jnp.float32)
    grad_s = (probs * (grad_p - row_dot)).astype(jnp.bfloat16)
    grad_q = (jnp.dot(grad_s, key_rows, preferred_element_type=jnp.float32) * scale).astype(jnp.bfloat16)
    grad_k = (jnp.dot(grad_s.T, query, preferred_element_type=jnp.float32) * scale).astype(jnp.bfloat16)
    grad_v = jnp.dot(probs_b.T, grad_out, preferred_element_type=jnp.float32).astype(jnp.bfloat16)
    return (grad_q, grad_k, grad_v)

def reference(hidden, out_cot, proj_in, proj_out, attn_out_w, queries, keys, values, dino):
    images = hidden.shape[0]
    length = hidden.shape[1]
    target = unit_target(dino).reshape(images * length, D_DINO)
    flat_hidden = hidden.reshape(images * length, D)
    pre_act = jnp.dot(flat_hidden, proj_in, preferred_element_type=jnp.float32)
    silu_out = jax.nn.silu(pre_act).astype(jnp.bfloat16)
    projected = jnp.dot(silu_out, proj_out, preferred_element_type=jnp.float32)
    cosine, grad_z = cosine_grad(projected, target)
    grad_silu = jnp.dot(grad_z, proj_out.T, preferred_element_type=jnp.float32)
    grad_pre = (grad_silu * silu_slope(pre_act)).astype(jnp.bfloat16)
    grad_repa = jnp.dot(grad_pre, proj_in.T, preferred_element_type=jnp.float32)
    grad_hidden = (out_cot.reshape(images * length, D).astype(jnp.float32) + grad_repa).astype(jnp.bfloat16)
    grad_attn = jnp.dot(grad_hidden, attn_out_w.T, preferred_element_type=jnp.float32).astype(jnp.bfloat16)

    def per_head(array):
        shaped = array.reshape(images, length, HEADS, HEAD_DIM)
        return jnp.transpose(shaped, (0, 2, 1, 3)).reshape(images * HEADS, length, HEAD_DIM)

    def back_layout(array):
        shaped = array.reshape(images, HEADS, length, HEAD_DIM)
        return jnp.transpose(shaped, (0, 2, 1, 3)).reshape(images, length, HEADS * HEAD_DIM)
    grad_q, grad_k, grad_v = lax.map(head_backward, (per_head(queries), per_head(keys), per_head(values), per_head(grad_attn)))
    return (cosine.reshape(images, length), back_layout(grad_q), back_layout(grad_k), back_layout(grad_v))
```

```python
import functools

import jax
import jax.numpy as jnp
from jax import lax
from jax.experimental import pallas as pl
from jax.experimental.pallas import tpu as pltpu
from jax.sharding import PartitionSpec as P

HEAD_DIM = 64
LANES = 128
LOSS_WEIGHT = 1000.0
EPS = 1e-06
F32 = jnp.float32
BF16 = jnp.bfloat16


def dot(a, b, dims=((1,), (0,))):
    return lax.dot_general(a, b, (dims, ((), ())), preferred_element_type=F32)


def cost(flops, nbytes, trans=0):
    return pl.CostEstimate(flops=int(flops), bytes_accessed=int(nbytes), transcendentals=int(trans))


def whole(shape):
    return pl.BlockSpec(shape, lambda *_: (0,) * len(shape))


def to_slots(arrays, parts):
    rows, cols = arrays[0].shape
    wide = cols // parts
    n = len(arrays)

    if wide % LANES:
        pieces = [a.reshape(rows, parts, wide) for a in arrays]
        return jnp.transpose(jnp.concatenate(pieces, axis=2), (1, 0, 2))

    def body(*refs):
        for at in range(n):
            refs[n][0, :, at * wide : (at + 1) * wide] = refs[at][...]

    return pl.pallas_call(
        body,
        grid=(parts,),
        in_specs=[pl.BlockSpec((rows, wide), lambda j: (0, j))] * n,
        out_specs=pl.BlockSpec((1, rows, n * wide), lambda j: (j, 0, 0)),
        out_shape=jax.ShapeDtypeStruct((parts, rows, n * wide), arrays[0].dtype),
        cost_estimate=cost(0, 4 * n * rows * cols),
        name="to_slots",
    )(*arrays)


def from_slots(chunks, outs):
    parts, rows, wide3 = chunks[0].shape
    wide = wide3 // outs
    n = len(chunks)

    if (n * wide) % LANES or wide % LANES:
        result = []
        for o in range(outs):
            pieces = [c[:, :, o * wide : (o + 1) * wide] for c in chunks]
            joined = jnp.transpose(jnp.stack(pieces, axis=2), (1, 0, 2, 3))
            result.append(joined.reshape(rows, parts * n * wide))
        return result

    def body(*refs):
        for at in range(n):
            for o in range(outs):
                refs[n + o][:, at * wide : (at + 1) * wide] = refs[at][
                    0, :, o * wide : (o + 1) * wide
                ]

    return pl.pallas_call(
        body,
        grid=(parts,),
        in_specs=[pl.BlockSpec((1, rows, wide3), lambda j: (j, 0, 0))] * n,
        out_specs=[pl.BlockSpec((rows, n * wide), lambda j: (0, j))] * outs,
        out_shape=[jax.ShapeDtypeStruct((rows, parts * n * wide), chunks[0].dtype)] * outs,
        cost_estimate=cost(0, 4 * n * parts * rows * wide3),
        name="from_slots",
    )(*chunks)


def unit_target(features):
    channels, tokens = features.shape

    def body(f_ref, o_ref):
        f = f_ref[...].astype(F32)
        shifted = f - jnp.mean(f, axis=0, keepdims=True)
        spread = jnp.mean(shifted * shifted, axis=0, keepdims=True)
        normed = shifted * lax.rsqrt(spread + EPS)
        total = jnp.sum(normed * normed, axis=0, keepdims=True)
        o_ref[...] = (normed * lax.rsqrt(total + EPS)).T

    return pl.pallas_call(
        body,
        out_shape=jax.ShapeDtypeStruct((tokens, channels), F32),
        cost_estimate=cost(8 * channels * tokens, 6 * channels * tokens),
        name="unit_target",
    )(features)


def cosine_grad(own, near, far, target):
    tokens, channels = own.shape

    def body(own_ref, near_ref, far_ref, t_ref, c_ref, g_ref):
        z = own_ref[...] + near_ref[...].astype(F32) + far_ref[...].astype(F32)
        t = t_ref[...]
        rinv = lax.rsqrt(jnp.sum(z * z, axis=-1, keepdims=True) + EPS)
        direction = z * rinv
        cosine = jnp.sum(direction * t, axis=-1, keepdims=True)
        c_ref[...] = cosine
        g_ref[...] = ((-LOSS_WEIGHT * rinv) * (t - cosine * direction)).astype(BF16)

    return pl.pallas_call(
        body,
        out_shape=[
            jax.ShapeDtypeStruct((tokens, 1), F32),
            jax.ShapeDtypeStruct((tokens, channels), BF16),
        ],
        cost_estimate=cost(10 * channels * tokens, 16 * channels * tokens),
        name="cosine_grad",
    )(own, near, far, target)


def hidden_block(units):
    return 256 if units % 256 == 0 else units


def projector(mine, other, w1, w2):
    tokens, width = mine.shape
    units = w1.shape[1]
    chans = w2.shape[1]
    blk = hidden_block(units)
    steps = units // blk

    def body(a_ref, b_ref, w1_ref, w2_ref, pre_ref, keep_ref, send_ref, rows, acc):
        step = pl.program_id(0)

        @pl.when(step == 0)
        def _():
            rows[:tokens] = a_ref[...]
            rows[tokens:] = b_ref[...]

        pre = dot(rows[...], w1_ref[...])
        pre_ref[...] = pre
        act = (pre / (1.0 + jnp.exp(-pre))).astype(BF16)
        part = dot(act, w2_ref[...])

        @pl.when(step == 0)
        def _():
            acc[...] = part

        @pl.when(step > 0)
        def _():
            acc[...] += part

        @pl.when(step == steps - 1)
        def _():
            keep_ref[...] = acc[:tokens]
            send_ref[...] = acc[tokens:].astype(BF16)

    return pl.pallas_call(
        body,
        grid=(steps,),
        in_specs=[
            whole((tokens, width)),
            whole((tokens, width)),
            pl.BlockSpec((width, blk), lambda s: (0, s)),
            pl.BlockSpec((blk, chans), lambda s: (s, 0)),
        ],
        out_specs=[
            pl.BlockSpec((2 * tokens, blk), lambda s: (0, s)),
            whole((tokens, chans)),
            whole((tokens, chans)),
        ],
        out_shape=[
            jax.ShapeDtypeStruct((2 * tokens, units), F32),
            jax.ShapeDtypeStruct((tokens, chans), F32),
            jax.ShapeDtypeStruct((tokens, chans), BF16),
        ],
        scratch_shapes=[pltpu.VMEM((2 * tokens, width), BF16), pltpu.VMEM((2 * tokens, chans), F32)],
        cost_estimate=cost(4 * tokens * units * (width + chans), 2 * units * (width + chans)),
        name="projector",
    )(mine, other, w1, w2)


def projector_back(mine, other, pre, w1, w2):
    tokens, chans = mine.shape
    width, units = w1.shape
    blk = hidden_block(units)
    steps = units // blk

    def body(a_ref, b_ref, pre_ref, w1_ref, w2_ref, keep_ref, send_ref, rows, acc):
        step = pl.program_id(0)

        @pl.when(step == 0)
        def _():
            rows[:tokens] = a_ref[...]
            rows[tokens:] = b_ref[...]

        grad = dot(rows[...], w2_ref[...], ((1,), (1,)))
        p = pre_ref[...]
        sigma = 1.0 / (1.0 + jnp.exp(-p))
        slope = sigma * (1.0 + p * (1.0 - sigma))
        part = dot((grad * slope).astype(BF16), w1_ref[...], ((1,), (1,)))

        @pl.when(step == 0)
        def _():
            acc[...] = part

        @pl.when(step > 0)
        def _():
            acc[...] += part

        @pl.when(step == steps - 1)
        def _():
            keep_ref[...] = acc[:tokens]
            send_ref[...] = acc[tokens:].astype(BF16)

    return pl.pallas_call(
        body,
        grid=(steps,),
        in_specs=[
            whole((tokens, chans)),
            whole((tokens, chans)),
            pl.BlockSpec((2 * tokens, blk), lambda s: (0, s)),
            pl.BlockSpec((width, blk), lambda s: (0, s)),
            pl.BlockSpec((blk, chans), lambda s: (s, 0)),
        ],
        out_specs=[whole((tokens, width)), whole((tokens, width))],
        out_shape=[
            jax.ShapeDtypeStruct((tokens, width), F32),
            jax.ShapeDtypeStruct((tokens, width), BF16),
        ],
        scratch_shapes=[pltpu.VMEM((2 * tokens, chans), BF16), pltpu.VMEM((2 * tokens, width), F32)],
        cost_estimate=cost(4 * tokens * units * (width + chans), 2 * units * (width + chans)),
        name="projector_back",
    )(mine, other, pre, w1, w2)


def attn_out_back(cot, own, near, far, weight, parts, wide, chunk):
    tokens, width = cot.shape
    chunks = weight.shape[0] // (parts * wide)
    group = max(1, min(parts, 256 // wide))
    steps = parts // group
    view = weight.reshape(parts, chunks, wide, width)

    def body(cot_ref, own_ref, near_ref, far_ref, w_ref, o_ref, rows):
        @pl.when(pl.program_id(0) == 0)
        def _():
            repa = own_ref[...] + near_ref[...].astype(F32) + far_ref[...].astype(F32)
            rows[...] = (cot_ref[...].astype(F32) + repa).astype(BF16)

        w = w_ref[...].reshape(group * wide, width)
        grad = dot(rows[...], w, ((1,), (1,))).astype(BF16)
        for at in range(group):
            o_ref[at] = grad[:, at * wide : (at + 1) * wide]

    return pl.pallas_call(
        body,
        grid=(steps,),
        in_specs=[
            whole((tokens, width)),
            whole((tokens, width)),
            whole((tokens, width)),
            whole((tokens, width)),
            pl.BlockSpec((group, None, wide, width), lambda s: (s, chunk, 0, 0)),
        ],
        out_specs=pl.BlockSpec((group, tokens, wide), lambda s: (s, 0, 0)),
        out_shape=jax.ShapeDtypeStruct((parts, tokens, wide), BF16),
        scratch_shapes=[pltpu.VMEM((tokens, width), BF16)],
        cost_estimate=cost(2 * tokens * parts * wide * width, 2 * parts * wide * width),
        name="attn_out_back",
    )(cot, own, near, far, view)


def query_block(length):
    return min(length, 256 if length <= 1024 else 128)


def attention_probs(q, k, v, at, wide):
    (q, q0), (k, k0), (v, v0) = q, k, v
    length = q.shape[0]
    blk = query_block(length)
    heads = wide // HEAD_DIM
    scale = HEAD_DIM**-0.5

    def body(q_ref, k_ref, v_ref, p_ref, a_ref):
        for h in range(heads):
            cols = slice(h * HEAD_DIM, (h + 1) * HEAD_DIM)
            scores = dot(k_ref[:, cols], q_ref[:, cols], ((1,), (1,)))
            top = jnp.max(scores, axis=0, keepdims=True)
            e = jnp.exp((scores - top) * scale)
            total = jnp.sum(e, axis=0, keepdims=True)
            probs = (e * (1.0 / total)).astype(BF16)
            p_ref[h] = probs
            a_ref[cols, :] = dot(v_ref[:, cols].T, probs)

    return pl.pallas_call(
        body,
        grid=(length // blk,),
        in_specs=[
            pl.BlockSpec((blk, wide), lambda i: (i, q0 + at)),
            pl.BlockSpec((length, wide), lambda i: (0, k0 + at)),
            pl.BlockSpec((length, wide), lambda i: (0, v0 + at)),
        ],
        out_specs=[
            pl.BlockSpec((heads, length, blk), lambda i: (0, 0, i)),
            pl.BlockSpec((wide, blk), lambda i: (0, i)),
        ],
        out_shape=[
            jax.ShapeDtypeStruct((heads, length, length), BF16),
            jax.ShapeDtypeStruct((wide, length), F32),
        ],
        cost_estimate=cost(
            16 * heads * length * length * HEAD_DIM,
            2 * heads * length * length,
            heads * length * length,
        ),
        name="attention_probs",
    )(q, k, v)


def attention_back(probs, attended, q, k, v, g, at, wide):
    (q, q0), (k, k0), (v, v0) = q, k, v
    length = q.shape[0]
    blk = query_block(length)
    heads = wide // HEAD_DIM
    steps = length // blk
    scale = HEAD_DIM**-0.5

    def body(p_ref, a_ref, q_ref, k_ref, v_ref, g_ref, o_ref, acc_k, acc_v):
        step = pl.program_id(0)

        @pl.when(step == 0)
        def _():
            acc_k[...] = jnp.zeros_like(acc_k)
            acc_v[...] = jnp.zeros_like(acc_v)

        grads_q = []
        for h in range(heads):
            cols = slice(h * HEAD_DIM, (h + 1) * HEAD_DIM)
            gh = g_ref[:, cols]
            pb = p_ref[h]
            grad_p = dot(v_ref[:, cols], gh, ((1,), (1,)))
            row_dot = jnp.sum(gh.astype(F32).T * a_ref[cols, :], axis=0, keepdims=True)
            grad_s = (pb.astype(F32) * (grad_p - row_dot)).astype(BF16)
            grads_q.append((dot(k_ref[:, cols].T, grad_s) * scale).T)
            acc_k[:, cols] += dot(grad_s, q_ref[:, cols])
            acc_v[:, cols] += dot(pb, gh)
        here = pl.multiple_of(step * blk, blk)
        o_ref[pl.ds(here, blk), :wide] = jnp.concatenate(grads_q, axis=1).astype(BF16)

        @pl.when(step == steps - 1)
        def _():
            o_ref[:, wide : 2 * wide] = (acc_k[...] * scale).astype(BF16)
            o_ref[:, 2 * wide :] = acc_v[...].astype(BF16)

    return pl.pallas_call(
        body,
        grid=(steps,),
        in_specs=[
            pl.BlockSpec((heads, length, blk), lambda i: (0, 0, i)),
            pl.BlockSpec((wide, blk), lambda i: (0, i)),
            pl.BlockSpec((blk, wide), lambda i: (i, q0 + at)),
            pl.BlockSpec((length, wide), lambda i: (0, k0 + at)),
            pl.BlockSpec((length, wide), lambda i: (0, v0 + at)),
            pl.BlockSpec((blk, wide), lambda i: (i, 0)),
        ],
        out_specs=whole((length, 3 * wide)),
        out_shape=jax.ShapeDtypeStruct((length, 3 * wide), BF16),
        scratch_shapes=[pltpu.VMEM((length, wide), F32), pltpu.VMEM((length, wide), F32)],
        cost_estimate=cost(
            32 * heads * length * length * HEAD_DIM, 2 * heads * length * length, 0
        ),
        name="attention_back",
    )(probs, attended, q, k, v, g)


def on_device(
    n_dp, n_seq, hidden, out_cot, proj_in, proj_out, attn_out_w, queries, keys, values, dino
):
    def swap(x, mask):
        return lax.ppermute(x, "dp", [(i, i ^ mask) for i in range(n_dp)])

    near = functools.partial(swap, mask=1)
    far = functools.partial(swap, mask=n_dp // 2)

    def exchange(x):
        return lax.all_to_all(x, "seq", split_axis=0, concat_axis=0, tiled=True)

    hidden, out_cot, dino = hidden[0], out_cot[0], dino[0]
    queries, keys, values = queries[0], keys[0], values[0]
    tokens = hidden.shape[0]
    length = tokens * n_seq
    per_dev = queries.shape[1] // n_seq
    wide = LANES if per_dev % LANES == 0 else HEAD_DIM
    blocks = per_dev // wide

    hid_far = far(hidden)
    hid_near = near(hidden)
    hid_diag = near(hid_far)

    feats = exchange(to_slots([dino], n_seq)).reshape(-1, tokens)
    target = unit_target(feats)

    if wide == LANES:
        qkv = exchange(to_slots([queries, keys, values], n_seq)).reshape(length, 3 * per_dev)
        q, k, v = ((qkv, i * blocks) for i in range(3))
    else:
        q, k, v = (
            (exchange(to_slots([a], n_seq)).reshape(length, per_dev), 0)
            for a in (queries, keys, values)
        )

    pre_own, keep_own, send_near = projector(hidden, hid_near, proj_in, proj_out)
    pre_far, keep_far, send_diag = projector(hid_far, hid_diag, proj_in, proj_out)
    got_diag = near(send_diag)
    got_near = near(send_near)
    got_far = far((keep_far + got_diag.astype(F32)).astype(BF16))
    cosine, grad_z = cosine_grad(keep_own, got_near, got_far, target)

    gz_far = far(grad_z)
    gz_near = near(grad_z)
    gz_diag = near(gz_far)
    keep_own, send_near = projector_back(grad_z, gz_near, pre_own, proj_in, proj_out)
    keep_far, send_diag = projector_back(gz_far, gz_diag, pre_far, proj_in, proj_out)
    got_diag = near(send_diag)
    got_near = near(send_near)
    got_far = far((keep_far + got_diag.astype(F32)).astype(BF16))

    forward = [attention_probs(q, k, v, at, wide) for at in range(blocks)]
    grads = [
        exchange(
            attn_out_back(out_cot, keep_own, got_near, got_far, attn_out_w, n_seq, wide, at)
        ).reshape(length, wide)
        for at in range(blocks)
    ]
    back = []
    for at in range(blocks):
        probs, attended = forward[at]
        both = attention_back(probs, attended, q, k, v, grads[at], at, wide)
        back.append(exchange(both.reshape(n_seq, tokens, 3 * wide)))
    outs = from_slots(back, 3)
    return (cosine.reshape(1, tokens), *(o[None] for o in outs))


def solution(mesh):
    in_specs = (
        P("dp", "seq", None),
        P("dp", "seq", None),
        P(None, "dp"),
        P("dp", None),
        P(),
        P("dp", "seq", None),
        P("dp", "seq", None),
        P("dp", "seq", None),
        P("dp", "seq", None),
    )
    out_specs = (P("dp", "seq"), P("dp", "seq", None), P("dp", "seq", None), P("dp", "seq", None))
    run = functools.partial(on_device, mesh.shape["dp"], mesh.shape["seq"])
    return jax.shard_map(run, mesh=mesh, in_specs=in_specs, out_specs=out_specs, check_vma=False)
```
